32 devices in a mesh: row: 4 (over x, core), col: 8 (over z, y).
Axes of the slice: x: 2, y: 2, z: 4, core: 2. Of those that a mesh axis runs over, the one named last changes fastest.
Arguments:
- vectors: float32 [32768, 128], P(('col', 'row')), may hold values from -6 to 6
- tile_values: bfloat16 [4, 8, 22, 512, 512], P('row', 'col'), may hold values from 0 to 1
- tile_rows: int32 [4, 8, 22], P('row', 'col'), may hold values from 0 to 15, as said below
- tile_cols: int32 [4, 8, 22], P('row', 'col'), may hold values from 0 to 7
- tile_count: int32 [4, 8], P('row', 'col'), may hold values from 1 to 22, as said below
- degrees: int32 [32768], replicated, may hold values from 16 to 255
Outputs:
- result: float32 [32768, 128], P(('row', 'col'))
The draws below stay inside these ranges and needn't reach their ends.
Inputs may be any that keep to these rules, and one draw needn't show every extreme that they name: `tile_rows`: within one device no two slots name the same pair of tile row and tile column. `tile_count`: some device has all 22 slots live.
All inputs are finite; a program needn't handle non-finite values.
Results may differ from the reference program's by a relative error of at most 0.0003.
Values sent between devices are 32-bit elements; how exact they have to be, the bound alone decides.
A program may use at most 128 MiB of HBM per device.

```python
import jax
import jax.numpy as jnp
from jax import lax

TS = 512
V = 128
TILES_DEV = 22
ROW_TILES = 16
COL_TILES = 8
NODES = 32768
N_ROW = 4
N_COL = 8


def tile_places(key):
    sub_key = jax.random.fold_in(key, 7)
    dev_keys = jax.random.split(sub_key, N_ROW * N_COL)

    def pick_places(dev_key):
        return jax.random.permutation(dev_key, ROW_TILES * COL_TILES)[:TILES_DEV]
    places = jax.vmap(pick_places)(dev_keys)
    return places.reshape(N_ROW, N_COL, TILES_DEV).astype(jnp.int32)


def draw_tile_rows(key, part):
    return (tile_places(key) // COL_TILES).astype(jnp.int32)


def draw_tile_cols(key, part):
    return (tile_places(key) % COL_TILES).astype(jnp.int32)


def draw_tile_count(key, part):
    first_key, second_key = jax.random.split(jax.random.fold_in(key, 11))
    draw_base = jax.random.randint(first_key, (N_ROW * N_COL,), 0, TILES_DEV)
    counts = 1 + draw_base * draw_base // TILES_DEV
    full_device = jax.random.randint(second_key, (), 0, N_ROW * N_COL)
    flat_counts = jnp.where(jnp.arange(N_ROW * N_COL) == full_device, TILES_DEV, counts)
    return flat_counts.reshape(N_ROW, N_COL).astype(jnp.int32)


def draw_degrees(key, part):
    first_key, second_key = jax.random.split(jax.random.fold_in(key, 13))
    exponent = jax.random.randint(first_key, (NODES,), 0, 4)
    low_end = jnp.left_shift(jnp.full((NODES,), 16, jnp.int32), exponent.astype(jnp.int32))
    offset_add = jax.random.randint(second_key, (NODES,), 0, low_end)
    return (low_end + offset_add).astype(jnp.int32)


def level_of(stream_key, extent, cuts, least, largest):
    loudness, own = 1.0, jax.random.fold_in(stream_key, 6)
    for position, shards_of in cuts:
        draws = jnp.exp(jax.random.uniform(jax.random.fold_in(own, position), (shards_of,), jnp.float32, least / len(cuts), largest / len(cuts)))
        loudness = loudness * jnp.repeat(draws, extent[position] // shards_of).reshape([-1 if axis == position else 1 for axis in range(len(extent))])
    return loudness


def noise(rng, shape, spread, bound, cuts=(), kind=jnp.bfloat16):
    entries = spread * jax.random.normal(rng, shape, jnp.float32)
    if cuts:
        entries = entries * level_of(rng, shape, cuts, -0.22, 0.18)
    return jnp.clip(entries, -bound, bound).astype(kind)


def setup_inputs(seed: int = 0) -> dict:
    splits = jax.random.split(jax.random.key(seed), 7)
    vectors = noise(splits[0], (NODES, V), 1.0, 6.0, ((0, 32),), jnp.float32)
    tile_values = jnp.clip(1.0 * jax.random.uniform(splits[1], (N_ROW, N_COL, TILES_DEV, TS, TS), jnp.float32) ** level_of(splits[1], (N_ROW, N_COL, TILES_DEV, TS, TS), ((0, 4), (1, 8)), -0.2, 0.2), 0.0, 1.0).astype(jnp.bfloat16)
    tile_rows = draw_tile_rows(jax.random.fold_in(splits[6], 71), 0)
    tile_cols = draw_tile_cols(jax.random.fold_in(splits[6], 71), 0)
    tile_count = draw_tile_count(jax.random.fold_in(splits[6], 71), 0)
    degrees = draw_degrees(jax.random.fold_in(splits[6], 71), 0)
    return {"vectors": vectors, "tile_values": tile_values, "tile_rows": tile_rows, "tile_cols": tile_cols, "tile_count": tile_count, "degrees": degrees}


def reference(vectors, tile_values, tile_rows, tile_cols, tile_count, degrees):
    inv_root = lax.rsqrt(degrees.astype(jnp.float32))
    scaled = (vectors * inv_root[:, None]).reshape(NODES // TS, TS, V)
    devices = N_ROW * N_COL
    device_ids = jnp.arange(devices, dtype=jnp.int32)
    slot_ids = jnp.arange(TILES_DEV, dtype=jnp.int32)

    def add_device(summed, device_item):
        tile_block, row_ids, col_ids, live_count, device_id = device_item
        row_block = device_id // N_COL
        col_block = device_id % N_COL
        chosen = scaled[(col_block * COL_TILES + col_ids).astype(jnp.int32)]
        contrib = jnp.einsum('kij,kjv->kiv', tile_block.astype(jnp.float32), chosen.astype(jnp.float32), precision=lax.Precision.HIGHEST)
        live_mask = (slot_ids < live_count).astype(jnp.float32)
        contrib = contrib * live_mask[:, None, None]
        summed = summed.at[(row_block * ROW_TILES + row_ids).astype(jnp.int32)].add(contrib)
        return (summed, None)
    start = jnp.zeros((NODES // TS, TS, V), jnp.float32)
    summed, _ = lax.scan(add_device, start, (tile_values.reshape(devices, TILES_DEV, TS, TS), tile_rows.reshape(devices, TILES_DEV), tile_cols.reshape(devices, TILES_DEV), tile_count.reshape(devices), device_ids))
    return summed.reshape(NODES, V) * inv_root[:, None]
```

```python
import functools

import jax
import jax.numpy as jnp
from jax import lax
from jax.experimental import pallas as pl
from jax.experimental.pallas import tpu as pltpu
from jax.sharding import PartitionSpec as P

MESH = pl.DeviceIdType.MESH


def inner_size(col_count):
    inner = 1
    while inner * inner * 4 <= col_count and col_count % (inner * 2) == 0:
        inner *= 2
    return inner


def kernel(
    dims,
    rows_s, cols_s, count_s, vec_ref, deg_ref, tiles_hbm, out_ref,
    tiles_v, gath, split_v, sums, inb, outb, prev_s, last_s,
    tile_sem, d_send, d_recv, m_send, m_recv, f_send, f_recv,
    i_send, i_recv, o_send, o_recv,
):
    R, A, B, piece, width, side, slots = dims
    C = A * B
    tpp = piece // side
    chips = R // 2
    me_row = lax.axis_index("row")
    me_col = lax.axis_index("col")
    chip, core = me_row // 2, me_row % 2
    mate = chip * 2 + (1 - core)
    a, b = me_col // B, me_col % B
    lanes = 128

    tile_copy = pltpu.make_async_copy(tiles_hbm.at[0, 0], tiles_v, tile_sem)
    tile_copy.start()

    def rdma(src, dst, ssem, rsem, where):
        return pltpu.make_async_remote_copy(
            src_ref=src, dst_ref=dst, send_sem=ssem, recv_sem=rsem,
            device_id=where, device_id_type=MESH,
        )

    barrier = pltpu.get_barrier_semaphore()

    def greet(where):
        pl.semaphore_signal(barrier, inc=1, device_id=where, device_id_type=MESH)

    greet({"row": mate})
    for j in range(1, chips):
        greet({"row": lax.rem(chip + j, chips) * 2 + core})
    conds = []
    if B > 1:
        conds += [(b > 0, me_col - 1), (b < B - 1, me_col + 1)]
    if A > 1:
        conds += [(a > 0, me_col - B), (a < A - 1, me_col + B)]
    for cond, other in conds:
        @pl.when(cond)
        def _(other=other):
            greet({"col": other})
    peers = jnp.int32(chips)
    for cond, other in conds:
        peers = peers + jnp.where(cond, 1, 0)
    pl.semaphore_wait(barrier, peers)

    def part(c):
        return pl.ds(c * side, side)

    directs, mates, forwards = {}, [], {}
    for c in range(tpp):
        for j in range(1, chips):
            dst = lax.rem(chip + j, chips) * 2 + core
            cp = rdma(vec_ref.at[part(c)], gath.at[me_row, part(c)],
                      d_send.at[j - 1, c], d_recv.at[j - 1, c], {"row": dst})
            cp.start()
            directs[j, c] = cp
    for c in range(tpp):
        cp = rdma(vec_ref.at[part(c)], gath.at[me_row, part(c)],
                  m_send.at[c], m_recv.at[c], {"row": mate})
        cp.start()
        mates.append(cp)

    count = count_s[0, 0]

    def link(k, _):
        rk = rows_s[0, 0, k]
        v = jnp.int32(slots)
        for j in range(slots):
            v = jnp.where((rows_s[0, 0, j] == rk) & (j < k), j, v)
        prev_s[k] = v
        return 0

    lax.fori_loop(0, slots, link, 0)

    def ends(r, _):
        v = jnp.int32(slots)
        for j in range(slots):
            v = jnp.where((rows_s[0, 0, j] == r) & (j < count), j, v)
        last_s[r] = v
        return 0

    lax.fori_loop(0, C * tpp, ends, 0)
    sums[slots] = jnp.zeros((side, width), jnp.float32)

    def factors(first):
        d = deg_ref[pl.ds(first, 1), :].astype(jnp.float32)
        return jnp.broadcast_to(lax.rsqrt(d), (lanes, lanes)).T

    col_first = me_col * (R * piece // lanes)

    def scale(get, r, c):
        def step(q, _):
            f = factors(col_first + (r * piece + c * side) // lanes + q)
            x = get(pl.ds(c * side + q * lanes, lanes)) * f
            hi = x.astype(jnp.bfloat16)
            lo = (x - hi.astype(jnp.float32)).astype(jnp.bfloat16)
            at = pl.ds(pl.multiple_of(q * lanes, lanes), lanes)
            split_v[r * tpp + c, at, :width] = hi
            split_v[r * tpp + c, at, width:] = lo
            return 0

        lax.fori_loop(0, side // lanes, step, 0)

    def landed(r, c, ssem, rsem):
        rdma(gath.at[r, part(c)], gath.at[r, part(c)], ssem, rsem, {"row": mate}).wait_recv()

    for c in range(tpp):
        scale(lambda s: vec_ref[s, :], me_row, c)
    for c in range(tpp):
        landed(mate, c, m_send.at[c], m_recv.at[c])
        scale(lambda s: gath[mate, s, :], mate, c)
    for c in range(tpp):
        for j in range(1, chips):
            src = lax.rem(chip - j + chips, chips) * 2 + core
            landed(src, c, d_send.at[j - 1, c], d_recv.at[j - 1, c])
            cp = rdma(gath.at[src, part(c)], gath.at[src, part(c)],
                      f_send.at[j - 1, c], f_recv.at[j - 1, c], {"row": mate})
            cp.start()
            forwards[j, c] = cp
            scale(lambda s, src=src: gath[src, s, :], src, c)
    for c in range(tpp):
        for j in range(1, chips):
            src = lax.rem(chip - j + chips, chips) * 2 + (1 - core)
            landed(src, c, f_send.at[j - 1, c], f_recv.at[j - 1, c])
            scale(lambda s, src=src: gath[src, s, :], src, c)

    tile_copy.wait()

    def product(k, _):
        both = jnp.dot(tiles_v[k], split_v[cols_s[0, 0, k]], preferred_element_type=jnp.float32)
        sums[k] = both[:, :width] + both[:, width:] + sums[prev_s[k]]
        return 0

    lax.fori_loop(0, slots, product, 0)

    order = sorted_table(A)

    def pick(s):
        v = jnp.int32(order[0][s])
        for i in range(1, A):
            v = jnp.where(a == i, order[i][s], v)
        return v

    def own(d, t, u):
        return sums[last_s[(d * B + t) * tpp + u]]

    def inner_steps(action):
        for s in range(A):
            d = pick(s)
            for dist in range(B - 1, 0, -1):
                for right in (True, False):
                    t = b + dist if right else b - dist
                    slot = t + 1 if right else t
                    to = me_col + 1 if right else me_col - 1
                    more = b > 0 if right else b < B - 1

                    @pl.when((t < B) if right else (t >= 0))
                    def _(d=d, t=t, slot=slot, to=to, more=more, dist=dist):
                        cp = rdma(inb.at[d, slot], inb.at[d, slot],
                                  i_send.at[d, slot], i_recv.at[d, slot], {"col": to})
                        action(cp, d, t, slot, more, dist < B - 1)

    def inner_send(cp, d, t, slot, more, can):
        if can:
            @pl.when(more)
            def _():
                cp.wait_recv()
                for u in range(tpp):
                    inb[d, slot, part(u)] = inb[d, slot, part(u)] + own(d, t, u)

            @pl.when(jnp.logical_not(more))
            def _():
                for u in range(tpp):
                    inb[d, slot, part(u)] = own(d, t, u)
        else:
            for u in range(tpp):
                inb[d, slot, part(u)] = own(d, t, u)
        cp.start()

    inner_steps(inner_send)

    near = jnp.where(b > 0, b + 1, 0)

    def inner_done(d):
        if B > 1:
            for cond, slot in ((b > 0, b + 1), (b < B - 1, b)):
                @pl.when(cond)
                def _(slot=slot):
                    rdma(inb.at[d, slot], inb.at[d, slot], i_send.at[d, slot],
                         i_recv.at[d, slot], {"row": mate}).wait_recv()
        if B > 2:
            @pl.when((b > 0) & (b < B - 1))
            def _():
                for u in range(tpp):
                    inb[d, b + 1, part(u)] = inb[d, b + 1, part(u)] + inb[d, b, part(u)]

    def here(d, u):
        v = own(d, b, u)
        if B > 1:
            v = v + inb[d, near, part(u)]
        return v

    def outer_copy(s):
        d = pick(s)
        right = d > a
        slot = jnp.where(right, d + 1, d)
        to = jnp.where(right, me_col + B, me_col - B)
        cp = rdma(outb.at[slot], outb.at[slot], o_send.at[slot], o_recv.at[slot], {"col": to})
        return d, right, slot, cp

    for s in range(A - 1):
        d, right, slot, cp = outer_copy(s)
        inner_done(d)
        more = (right & (a > 0)) | (jnp.logical_not(right) & (a < A - 1))

        @pl.when(more)
        def _(d=d, slot=slot, cp=cp):
            cp.wait_recv()
            for u in range(tpp):
                outb[slot, part(u)] = outb[slot, part(u)] + here(d, u)

        @pl.when(jnp.logical_not(more))
        def _(d=d, slot=slot):
            for u in range(tpp):
                outb[slot, part(u)] = here(d, u)

        cp.start()

    inner_done(a)
    for u in range(tpp):
        out_ref[part(u), :] = here(a, u)
    if A > 1:
        for cond, slot in ((a > 0, a + 1), (a < A - 1, a)):
            @pl.when(cond)
            def _(slot=slot):
                rdma(outb.at[slot], outb.at[slot], o_send.at[slot],
                     o_recv.at[slot], {"row": mate}).wait_recv()
                for u in range(tpp):
                    out_ref[part(u), :] = out_ref[part(u), :] + outb[slot, part(u)]
    out_first = (me_row * C + me_col) * (piece // lanes)
    for q in range(piece // lanes):
        at = pl.ds(q * lanes, lanes)
        out_ref[at, :] = out_ref[at, :] * factors(out_first + q)

    for group in (directs.values(), mates, forwards.values()):
        for cp in group:
            cp.wait_send()
    inner_steps(lambda cp, *rest: cp.wait_send())
    for s in range(A - 1):
        outer_copy(s)[-1].wait_send()


def sorted_table(count):
    return [sorted(range(count), key=lambda d: (-abs(d - i), -d)) for i in range(count)]


def body(vectors, tile_values, tile_rows, tile_cols, tile_count, degrees):
    R = lax.axis_size("row")
    C = lax.axis_size("col")
    piece, width = vectors.shape
    side = tile_values.shape[-1]
    slots = tile_values.shape[2]
    B = inner_size(C)
    A = C // B
    tpp = piece // side
    chips = R // 2
    dims = (R, A, B, piece, width, side, slots)
    vmem = pl.BlockSpec(memory_space=pltpu.VMEM)
    smem = pl.BlockSpec(memory_space=pltpu.SMEM)
    dma = pltpu.SemaphoreType.DMA
    f32 = jnp.float32
    far = max(chips - 1, 1)
    return pl.pallas_call(
        functools.partial(kernel, dims),
        out_shape=jax.ShapeDtypeStruct((piece, width), f32),
        in_specs=[smem, smem, smem, vmem, vmem, pl.BlockSpec(memory_space=pl.ANY)],
        out_specs=vmem,
        scratch_shapes=[
            pltpu.VMEM((slots, side, side), tile_values.dtype),
            pltpu.VMEM((R, piece, width), f32),
            pltpu.VMEM((R * tpp, side, 2 * width), jnp.bfloat16),
            pltpu.VMEM((slots + 1, side, width), f32),
            pltpu.VMEM((A, B + 1, piece, width), f32),
            pltpu.VMEM((A + 1, piece, width), f32),
            pltpu.SMEM((slots,), jnp.int32),
            pltpu.SMEM((C * tpp,), jnp.int32),
            dma,
            dma((far, tpp)), dma((far, tpp)),
            dma((tpp,)), dma((tpp,)),
            dma((far, tpp)), dma((far, tpp)),
            dma((A, B + 1)), dma((A, B + 1)),
            dma((A + 1,)), dma((A + 1,)),
        ],
        compiler_params=pltpu.CompilerParams(
            collective_id=0, has_side_effects=True, vmem_limit_bytes=67043328
        ),
    )(tile_rows, tile_cols, tile_count, vectors, degrees.reshape(-1, 128), tile_values)


def solution(mesh):
    placed = (
        P(("col", "row"), None),
        P("row", "col", None, None, None),
        P("row", "col", None),
        P("row", "col", None),
        P("row", "col"),
        P(),
    )
    return jax.shard_map(
        body, mesh=mesh, in_specs=placed, out_specs=P(("row", "col"), None), check_vma=False
    )
```

```python
import functools

import jax
import jax.numpy as jnp
from jax import lax
from jax.experimental import pallas as pl
from jax.experimental.pallas import tpu as pltpu
from jax.sharding import PartitionSpec as P

MESH = pl.DeviceIdType.MESH


def inner_size(col_count):
    inner = 1
    while inner * inner * 4 <= col_count and col_count % (inner * 2) == 0:
        inner *= 2
    return inner


def kernel(
    dims,
    rows_s, cols_s, count_s, vec_ref, deg_ref, tiles_hbm, out_ref,
    tiles_v, gath, split_v, sums, inb, outb, zb, yb, prev_s, last_s,
    tile_sem, d_send, d_recv, m_send, m_recv, f_send, f_recv,
    i_send, i_recv, o_send, o_recv, z_send, z_recv, y_send, y_recv,
):
    R, A, B, piece, width, side, slots = dims
    C = A * B
    tpp = piece // side
    chips = R // 2
    me_row = lax.axis_index("row")
    me_col = lax.axis_index("col")
    chip, core = me_row // 2, me_row % 2
    mate = chip * 2 + (1 - core)
    a, b = me_col // B, me_col % B
    lanes = 128

    tile_copy = pltpu.make_async_copy(tiles_hbm.at[0, 0], tiles_v, tile_sem)
    tile_copy.start()

    def rdma(src, dst, ssem, rsem, where):
        return pltpu.make_async_remote_copy(
            src_ref=src, dst_ref=dst, send_sem=ssem, recv_sem=rsem,
            device_id=where, device_id_type=MESH,
        )

    barrier = pltpu.get_barrier_semaphore()

    def greet(where):
        pl.semaphore_signal(barrier, inc=1, device_id=where, device_id_type=MESH)

    greet({"row": mate})
    for j in range(1, chips):
        greet({"row": lax.rem(chip + j, chips) * 2 + core})
    conds = []
    if B > 1:
        conds += [(b > 0, me_col - 1), (b < B - 1, me_col + 1)]
    if A > 1:
        conds += [(a > 0, me_col - B), (a < A - 1, me_col + B)]
    for cond, other in conds:
        @pl.when(cond)
        def _(other=other):
            greet({"col": other})
    peers = jnp.int32(chips)
    for cond, other in conds:
        peers = peers + jnp.where(cond, 1, 0)
    pl.semaphore_wait(barrier, peers)

    def part(c):
        return pl.ds(c * side, side)

    directs, mates, forwards = {}, [], {}
    for c in range(tpp):
        for j in range(1, chips):
            dst = lax.rem(chip + j, chips) * 2 + core
            cp = rdma(vec_ref.at[part(c)], gath.at[me_row, part(c)],
                      d_send.at[j - 1, c], d_recv.at[j - 1, c], {"row": dst})
            cp.start()
            directs[j, c] = cp
    for c in range(tpp):
        cp = rdma(vec_ref.at[part(c)], gath.at[me_row, part(c)],
                  m_send.at[c], m_recv.at[c], {"row": mate})
        cp.start()
        mates.append(cp)

    count = count_s[0, 0]

    def link(k, _):
        rk = rows_s[0, 0, k]
        v = jnp.int32(slots)
        for j in range(slots):
            v = jnp.where((rows_s[0, 0, j] == rk) & (j < k), j, v)
        prev_s[k] = v
        return 0

    lax.fori_loop(0, slots, link, 0)

    def ends(r, _):
        v = jnp.int32(slots)
        for j in range(slots):
            v = jnp.where((rows_s[0, 0, j] == r) & (j < count), j, v)
        last_s[r] = v
        return 0

    lax.fori_loop(0, C * tpp, ends, 0)
    sums[slots] = jnp.zeros((side, width), jnp.float32)

    def factors(first):
        d = deg_ref[pl.ds(first, 1), :].astype(jnp.float32)
        return jnp.broadcast_to(lax.rsqrt(d), (lanes, lanes)).T

    col_first = me_col * (R * piece // lanes)

    def scale(get, r, c):
        def step(q, _):
            f = factors(col_first + (r * piece + c * side) // lanes + q)
            x = get(pl.ds(c * side + q * lanes, lanes)) * f
            hi = x.astype(jnp.bfloat16)
            lo = (x - hi.astype(jnp.float32)).astype(jnp.bfloat16)
            at = pl.ds(pl.multiple_of(q * lanes, lanes), lanes)
            split_v[r * tpp + c, at, :width] = hi
            split_v[r * tpp + c, at, width:] = lo
            return 0

        lax.fori_loop(0, side // lanes, step, 0)

    def landed(r, c, ssem, rsem):
        rdma(gath.at[r, part(c)], gath.at[r, part(c)], ssem, rsem, {"row": mate}).wait_recv()

    for c in range(tpp):
        scale(lambda s: vec_ref[s, :], me_row, c)
    for c in range(tpp):
        landed(mate, c, m_send.at[c], m_recv.at[c])
        scale(lambda s: gath[mate, s, :], mate, c)
    for c in range(tpp):
        for j in range(1, chips):
            src = lax.rem(chip - j + chips, chips) * 2 + core
            landed(src, c, d_send.at[j - 1, c], d_recv.at[j - 1, c])
            cp = rdma(gath.at[src, part(c)], gath.at[src, part(c)],
                      f_send.at[j - 1, c], f_recv.at[j - 1, c], {"row": mate})
            cp.start()
            forwards[j, c] = cp
            scale(lambda s, src=src: gath[src, s, :], src, c)
    for c in range(tpp):
        for j in range(1, chips):
            src = lax.rem(chip - j + chips, chips) * 2 + (1 - core)
            landed(src, c, f_send.at[j - 1, c], f_recv.at[j - 1, c])
            scale(lambda s, src=src: gath[src, s, :], src, c)

    tile_copy.wait()

    def product(k, _):
        both = jnp.dot(tiles_v[k], split_v[cols_s[0, 0, k]], preferred_element_type=jnp.float32)
        sums[k] = both[:, :width] + both[:, width:] + sums[prev_s[k]]
        return 0

    lax.fori_loop(0, slots, product, 0)

    order = sorted_table(A)
    cut = side - zb.shape[2]
    head = [(u, u * side, 0, side if u < tpp - 1 else cut) for u in range(tpp)]
    tail = (tpp - 1) * side + cut
    tail_rows = side - cut

    def pick(s):
        v = jnp.int32(order[0][s])
        for i in range(1, A):
            v = jnp.where(a == i, order[i][s], v)
        return v

    def own(d, t, u, n):
        return sums[last_s[(d * B + t) * tpp + u], :n]

    def own_tail(d, t):
        return sums[last_s[(d * B + t) * tpp + tpp - 1], cut:]

    def line(pos, size, stride, dist, action):
        for right in (True, False):
            t = pos + dist if right else pos - dist
            slot = t + 1 if right else t
            to = me_col + stride if right else me_col - stride
            more = pos > 0 if right else pos < size - 1

            @pl.when((t < size) if right else (t >= 0))
            def _(t=t, slot=slot, to=to, more=more):
                action(t, slot, to, more, dist < size - 1)

    def add_and_send(cp, more, can, store):
        if can:
            @pl.when(more)
            def _():
                cp.wait_recv()
                store(True)

            @pl.when(jnp.logical_not(more))
            def _():
                store(False)
        else:
            store(False)
        cp.start()

    def arrive(pos, size, ref, ssem, rsem, fold):
        if size > 1:
            for cond, slot in ((pos > 0, pos + 1), (pos < size - 1, pos)):
                @pl.when(cond)
                def _(slot=slot):
                    rdma(ref(slot), ref(slot), ssem(slot), rsem(slot), {"row": mate}).wait_recv()
        if size > 2:
            @pl.when((pos > 0) & (pos < size - 1))
            def _():
                fold(pos + 1, pos)

    near = jnp.where(b > 0, b + 1, 0)
    near_a = jnp.where(a > 0, a + 1, 0)

    def inner_copy(d, slot, to):
        at = inb.at[d, slot]
        return rdma(at, at, i_send.at[d, slot], i_recv.at[d, slot], {"col": to})

    def inner_send(d):
        def action(t, slot, to, more, can):
            def store(add):
                for u, at, _, n in head:
                    rows = pl.ds(at, n)
                    v = own(d, t, u, n)
                    inb[d, slot, rows] = inb[d, slot, rows] + v if add else v

            add_and_send(inner_copy(d, slot, to), more, can, store)
        return action

    def inner_done(d):
        def fold(x, y):
            inb[d, x] = inb[d, x] + inb[d, y]

        arrive(b, B, lambda q: inb.at[d, q], lambda q: i_send.at[d, q],
               lambda q: i_recv.at[d, q], fold)

    def here(d, u, at, n):
        v = own(d, b, u, n)
        if B > 1:
            v = v + inb[d, near, pl.ds(at, n)]
        return v

    def outer_copy(s):
        d = pick(s)
        right = d > a
        slot = jnp.where(right, d + 1, d)
        to = jnp.where(right, me_col + B, me_col - B)
        cp = rdma(outb.at[slot], outb.at[slot], o_send.at[slot], o_recv.at[slot], {"col": to})
        return d, right, slot, cp

    def outer_step(s):
        d, right, slot, cp = outer_copy(s)
        inner_done(d)
        more = (right & (a > 0)) | (jnp.logical_not(right) & (a < A - 1))

        def store(add):
            for u, at, _, n in head:
                rows = pl.ds(at, n)
                v = here(d, u, at, n)
                outb[slot, rows] = outb[slot, rows] + v if add else v

        add_and_send(cp, more, True, store)

    def zcopy(slot, to):
        return rdma(zb.at[slot], zb.at[slot], z_send.at[slot], z_recv.at[slot], {"col": to})

    def zsend(d, slot, to, more, can):
        def store(add):
            for t in range(B):
                v = own_tail(d, t)
                zb[slot, t] = zb[slot, t] + v if add else v

        add_and_send(zcopy(slot, to), more, can, store)

    def zhere(t):
        v = own_tail(a, t)
        if A > 1:
            v = v + zb[near_a, t]
        return v

    def ycopy(slot, to):
        return rdma(yb.at[slot], yb.at[slot], y_send.at[slot], y_recv.at[slot], {"col": to})

    def ysend(t, slot, to, more, can):
        def store(add):
            v = zhere(t)
            yb[slot] = yb[slot] + v if add else v

        add_and_send(ycopy(slot, to), more, can, store)

    def zfold(x, y):
        zb[x] = zb[x] + zb[y]

    def yfold(x, y):
        yb[x] = yb[x] + yb[y]

    def tail_turn():
        arrive(a, A, lambda q: zb.at[q], lambda q: z_send.at[q], lambda q: z_recv.at[q], zfold)
        for dist in range(B - 1, 0, -1):
            line(b, B, 1, dist, ysend)

    if A > 1:
        line(a, A, B, A - 1, zsend)
    for s in range(A):
        for dist in range(B - 1, 0, -1):
            line(b, B, 1, dist, inner_send(pick(s)))
    for dist in range(A - 2, 1, -1):
        line(a, A, B, dist, zsend)
    turn = min(1, A - 2)
    for s in range(A - 1):
        outer_step(s)
        if s == 0 and A > 2:
            line(a, A, B, 1, zsend)
        if s == turn:
            tail_turn()
    if A == 1:
        tail_turn()

    inner_done(a)
    for u, at, _, n in head:
        out_ref[pl.ds(at, n), :] = here(a, u, at, n)
    if A > 1:
        for cond, slot in ((a > 0, a + 1), (a < A - 1, a)):
            @pl.when(cond)
            def _(slot=slot):
                rdma(outb.at[slot], outb.at[slot], o_send.at[slot],
                     o_recv.at[slot], {"row": mate}).wait_recv()
                out_ref[pl.ds(0, tail), :] = out_ref[pl.ds(0, tail), :] + outb[slot]
    arrive(b, B, lambda q: yb.at[q], lambda q: y_send.at[q], lambda q: y_recv.at[q], yfold)
    last = zhere(b)
    if B > 1:
        last = last + yb[near]
    out_ref[pl.ds(tail, tail_rows), :] = last
    out_first = (me_row * C + me_col) * (piece // lanes)
    for q in range(piece // lanes):
        at = pl.ds(q * lanes, lanes)
        out_ref[at, :] = out_ref[at, :] * factors(out_first + q)

    for group in (directs.values(), mates, forwards.values()):
        for cp in group:
            cp.wait_send()
    for dist in range(A - 1, 0, -1):
        line(a, A, B, dist, lambda t, slot, to, *rest: zcopy(slot, to).wait_send())
    for dist in range(B - 1, 0, -1):
        line(b, B, 1, dist, lambda t, slot, to, *rest: ycopy(slot, to).wait_send())
        for s in range(A):
            d = pick(s)
            line(b, B, 1, dist, lambda t, slot, to, *rest, d=d: inner_copy(d, slot, to).wait_send())
    for s in range(A - 1):
        outer_copy(s)[-1].wait_send()


def sorted_table(count):
    return [sorted(range(count), key=lambda d: (-abs(d - i), -d)) for i in range(count)]


def body(vectors, tile_values, tile_rows, tile_cols, tile_count, degrees):
    R = lax.axis_size("row")
    C = lax.axis_size("col")
    piece, width = vectors.shape
    side = tile_values.shape[-1]
    slots = tile_values.shape[2]
    B = inner_size(C)
    A = C // B
    tpp = piece // side
    chips = R // 2
    dims = (R, A, B, piece, width, side, slots)
    vmem = pl.BlockSpec(memory_space=pltpu.VMEM)
    smem = pl.BlockSpec(memory_space=pltpu.SMEM)
    dma = pltpu.SemaphoreType.DMA
    f32 = jnp.float32
    far = max(chips - 1, 1)
    tail_rows = -(-piece // 96) * 16
    return pl.pallas_call(
        functools.partial(kernel, dims),
        out_shape=jax.ShapeDtypeStruct((piece, width), f32),
        in_specs=[smem, smem, smem, vmem, vmem, pl.BlockSpec(memory_space=pl.ANY)],
        out_specs=vmem,
        scratch_shapes=[
            pltpu.VMEM((slots, side, side), tile_values.dtype),
            pltpu.VMEM((R, piece, width), f32),
            pltpu.VMEM((R * tpp, side, 2 * width), jnp.bfloat16),
            pltpu.VMEM((slots + 1, side, width), f32),
            pltpu.VMEM((A, B + 1, piece - tail_rows, width), f32),
            pltpu.VMEM((A + 1, piece - tail_rows, width), f32),
            pltpu.VMEM((A + 1, B, tail_rows, width), f32),
            pltpu.VMEM((B + 1, tail_rows, width), f32),
            pltpu.SMEM((slots,), jnp.int32),
            pltpu.SMEM((C * tpp,), jnp.int32),
            dma,
            dma((far, tpp)), dma((far, tpp)),
            dma((tpp,)), dma((tpp,)),
            dma((far, tpp)), dma((far, tpp)),
            dma((A, B + 1)), dma((A, B + 1)),
            dma((A + 1,)), dma((A + 1,)),
            dma((A + 1,)), dma((A + 1,)),
            dma((B + 1,)), dma((B + 1,)),
        ],
        compiler_params=pltpu.CompilerParams(
            collective_id=0, has_side_effects=True, vmem_limit_bytes=67043328
        ),
    )(tile_rows, tile_cols, tile_count, vectors, degrees.reshape(-1, 128), tile_values)


def solution(mesh):
    placed = (
        P(("col", "row"), None),
        P("row", "col", None, None, None),
        P("row", "col", None),
        P("row", "col", None),
        P("row", "col"),
        P(),
    )
    return jax.shard_map(
        body, mesh=mesh, in_specs=placed, out_specs=P(("row", "col"), None), check_vma=False
    )
```

```python
import functools

import jax
import jax.numpy as jnp
from jax import lax
from jax.experimental import pallas as pl
from jax.experimental.pallas import tpu as pltpu
from jax.sharding import PartitionSpec as P

MESH = pl.DeviceIdType.MESH


def inner_size(col_count):
    inner = 1
    while inner * inner * 4 <= col_count and col_count % (inner * 2) == 0:
        inner *= 2
    return inner


def kernel(
    dims,
    rows_s, cols_s, count_s, vec_ref, deg_ref, tiles_hbm, out_ref,
    tiles_v, gath, split_v, sums, inb, outb, zb, yb, prev_s, last_s,
    tile_sem, vec_sem, d_send, d_recv, m_send, m_recv, f_send, f_recv,
    i_send, i_recv, o_send, o_recv, z_send, z_recv, y_send, y_recv,
):
    R, A, B, piece, width, side, slots = dims
    C = A * B
    tpp = piece // side
    chips = R // 2
    me_row = lax.axis_index("row")
    me_col = lax.axis_index("col")
    chip, core = me_row // 2, me_row % 2
    mate = chip * 2 + (1 - core)
    a, b = me_col // B, me_col % B
    lanes = 128

    tile_copy = pltpu.make_async_copy(tiles_hbm.at[0, 0], tiles_v, tile_sem)
    tile_copy.start()

    def rdma(src, dst, ssem, rsem, where):
        return pltpu.make_async_remote_copy(
            src_ref=src, dst_ref=dst, send_sem=ssem, recv_sem=rsem,
            device_id=where, device_id_type=MESH,
        )

    barrier = pltpu.get_barrier_semaphore()

    def greet(where):
        pl.semaphore_signal(barrier, inc=1, device_id=where, device_id_type=MESH)

    greet({"row": mate})
    for j in range(1, chips):
        greet({"row": lax.rem(chip + j, chips) * 2 + core})
    conds = []
    if B > 1:
        conds += [(b > 0, me_col - 1), (b < B - 1, me_col + 1)]
    if A > 1:
        conds += [(a > 0, me_col - B), (a < A - 1, me_col + B)]
    for cond, other in conds:
        @pl.when(cond)
        def _(other=other):
            greet({"col": other})
    peers = jnp.int32(chips)
    for cond, other in conds:
        peers = peers + jnp.where(cond, 1, 0)
    pl.semaphore_wait(barrier, peers)

    def part(c):
        return pl.ds(c * side, side)

    directs, mates, forwards = {}, [], {}
    for c in range(tpp):
        for j in range(1, chips):
            dst = lax.rem(chip + j, chips) * 2 + core
            cp = rdma(vec_ref.at[part(c)], gath.at[me_row, part(c)],
                      d_send.at[j - 1, c], d_recv.at[j - 1, c], {"row": dst})
            cp.start()
            directs[j, c] = cp
    for c in range(tpp):
        cp = rdma(vec_ref.at[part(c)], gath.at[me_row, part(c)],
                  m_send.at[c], m_recv.at[c], {"row": mate})
        cp.start()
        mates.append(cp)

    vec_copy = pltpu.make_async_copy(vec_ref, gath.at[me_row], vec_sem)
    vec_copy.start()

    count = count_s[0, 0]

    def link(k, _):
        rk = rows_s[0, 0, k]
        v = jnp.int32(slots)
        for j in range(slots):
            v = jnp.where((rows_s[0, 0, j] == rk) & (j < k), j, v)
        prev_s[k] = v
        return 0

    lax.fori_loop(0, slots, link, 0)

    def ends(r, _):
        v = jnp.int32(slots)
        for j in range(slots):
            v = jnp.where((rows_s[0, 0, j] == r) & (j < count), j, v)
        last_s[r] = v
        return 0

    lax.fori_loop(0, C * tpp, ends, 0)
    sums[slots] = jnp.zeros((side, width), jnp.float32)

    def factors(first):
        d = deg_ref[pl.ds(first, 1), :].astype(jnp.float32)
        return jnp.broadcast_to(lax.rsqrt(d), (lanes, lanes)).T

    col_first = me_col * (R * piece // lanes)

    def scale(get, r, c):
        def step(q, _):
            f = factors(col_first + (r * piece + c * side) // lanes + q)
            x = get(pl.ds(c * side + q * lanes, lanes)) * f
            hi = x.astype(jnp.bfloat16)
            lo = (x - hi.astype(jnp.float32)).astype(jnp.bfloat16)
            at = pl.ds(pl.multiple_of(q * lanes, lanes), lanes)
            split_v[r * tpp + c, at, :width] = hi
            split_v[r * tpp + c, at, width:] = lo
            return 0

        lax.fori_loop(0, side // lanes, step, 0)

    def landed(r, c, ssem, rsem):
        rdma(gath.at[r, part(c)], gath.at[r, part(c)], ssem, rsem, {"row": mate}).wait_recv()

    vec_copy.wait()
    for c in range(tpp):
        scale(lambda s: gath[me_row, s, :], me_row, c)
    for c in range(tpp):
        landed(mate, c, m_send.at[c], m_recv.at[c])
        scale(lambda s: gath[mate, s, :], mate, c)
    for c in range(tpp):
        for j in range(1, chips):
            src = lax.rem(chip - j + chips, chips) * 2 + core
            landed(src, c, d_send.at[j - 1, c], d_recv.at[j - 1, c])
            cp = rdma(gath.at[src, part(c)], gath.at[src, part(c)],
                      f_send.at[j - 1, c], f_recv.at[j - 1, c], {"row": mate})
            cp.start()
            forwards[j, c] = cp
            scale(lambda s, src=src: gath[src, s, :], src, c)
    for c in range(tpp):
        for j in range(1, chips):
            src = lax.rem(chip - j + chips, chips) * 2 + (1 - core)
            landed(src, c, f_send.at[j - 1, c], f_recv.at[j - 1, c])
            scale(lambda s, src=src: gath[src, s, :], src, c)

    tile_copy.wait()

    def products(lo, n):
        def product(k, _):
            both = jnp.dot(tiles_v[k, lo:lo + n], split_v[cols_s[0, 0, k]],
                           preferred_element_type=jnp.float32)
            old = sums[prev_s[k], lo:lo + n]
            sums[k, lo:lo + n] = both[:, :width] + both[:, width:] + old
            return 0

        lax.fori_loop(0, slots, product, 0)

    order = sorted_table(A)
    cut = side - zb.shape[2]
    tail = (tpp - 1) * side + cut
    tail_rows = side - cut
    early = [(u, u * tail_rows, cut, tail_rows) for u in range(tpp - 1)]
    late_at = (tpp - 1) * tail_rows
    late = [(u, late_at + u * cut, 0, cut) for u in range(tpp)]
    spans = [(late_at, tpp * cut, late)]
    if early:
        spans = [(0, late_at, early)] + spans

    def pick(s):
        v = jnp.int32(order[0][s])
        for i in range(1, A):
            v = jnp.where(a == i, order[i][s], v)
        return v

    def own(d, t, u, lo, n):
        return sums[last_s[(d * B + t) * tpp + u], lo:lo + n]

    def own_tail(d, t):
        return sums[last_s[(d * B + t) * tpp + tpp - 1], cut:]

    def line(pos, size, stride, dist, action):
        for right in (True, False):
            t = pos + dist if right else pos - dist
            slot = t + 1 if right else t
            to = me_col + stride if right else me_col - stride
            more = pos > 0 if right else pos < size - 1

            @pl.when((t < size) if right else (t >= 0))
            def _(t=t, slot=slot, to=to, more=more):
                action(t, slot, to, more, dist < size - 1)

    def add_and_send(cp, more, can, store):
        if can:
            @pl.when(more)
            def _():
                cp.wait_recv()
                store(True)

            @pl.when(jnp.logical_not(more))
            def _():
                store(False)
        else:
            store(False)
        cp.start()

    def arrive(pos, size, ref, ssem, rsem, fold):
        if size > 1:
            for cond, slot in ((pos > 0, pos + 1), (pos < size - 1, pos)):
                @pl.when(cond)
                def _(slot=slot):
                    rdma(ref(slot), ref(slot), ssem(slot), rsem(slot), {"row": mate}).wait_recv()
        if size > 2:
            @pl.when((pos > 0) & (pos < size - 1))
            def _():
                fold(pos + 1, pos)

    near = jnp.where(b > 0, b + 1, 0)
    near_a = jnp.where(a > 0, a + 1, 0)

    def inner_copy(h, d, slot, to):
        at = inb.at[d, slot, pl.ds(*spans[h][:2])]
        return rdma(at, at, i_send.at[h, d, slot], i_recv.at[h, d, slot], {"col": to})

    def inner_send(h, d):
        def action(t, slot, to, more, can):
            def store(add):
                for u, at, lo, n in spans[h][2]:
                    rows = pl.ds(at, n)
                    v = own(d, t, u, lo, n)
                    inb[d, slot, rows] = inb[d, slot, rows] + v if add else v

            add_and_send(inner_copy(h, d, slot, to), more, can, store)
        return action

    def inner_done(h, d):
        rows = pl.ds(*spans[h][:2])

        def fold(x, y):
            inb[d, x, rows] = inb[d, x, rows] + inb[d, y, rows]

        arrive(b, B, lambda q: inb.at[d, q, rows], lambda q: i_send.at[h, d, q],
               lambda q: i_recv.at[h, d, q], fold)

    def here(d, u, at, lo, n):
        v = own(d, b, u, lo, n)
        if B > 1:
            v = v + inb[d, near, pl.ds(at, n)]
        return v

    def outer_copy(h, s):
        d = pick(s)
        right = d > a
        slot = jnp.where(right, d + 1, d)
        to = jnp.where(right, me_col + B, me_col - B)
        at = outb.at[slot, pl.ds(*spans[h][:2])]
        return d, right, slot, rdma(at, at, o_send.at[h, slot], o_recv.at[h, slot], {"col": to})

    def outer_step(h, s):
        d, right, slot, cp = outer_copy(h, s)
        inner_done(h, d)
        more = (right & (a > 0)) | (jnp.logical_not(right) & (a < A - 1))

        def store(add):
            for u, at, lo, n in spans[h][2]:
                rows = pl.ds(at, n)
                v = here(d, u, at, lo, n)
                outb[slot, rows] = outb[slot, rows] + v if add else v

        add_and_send(cp, more, True, store)

    def zcopy(slot, to):
        return rdma(zb.at[slot], zb.at[slot], z_send.at[slot], z_recv.at[slot], {"col": to})

    def zsend(d, slot, to, more, can):
        def store(add):
            for t in range(B):
                v = own_tail(d, t)
                zb[slot, t] = zb[slot, t] + v if add else v

        add_and_send(zcopy(slot, to), more, can, store)

    def zhere(t):
        v = own_tail(a, t)
        if A > 1:
            v = v + zb[near_a, t]
        return v

    def ycopy(slot, to):
        return rdma(yb.at[slot], yb.at[slot], y_send.at[slot], y_recv.at[slot], {"col": to})

    def ysend(t, slot, to, more, can):
        def store(add):
            v = zhere(t)
            yb[slot] = yb[slot] + v if add else v

        add_and_send(ycopy(slot, to), more, can, store)

    def zfold(x, y):
        zb[x] = zb[x] + zb[y]

    def yfold(x, y):
        yb[x] = yb[x] + yb[y]

    def tail_turn():
        arrive(a, A, lambda q: zb.at[q], lambda q: z_send.at[q], lambda q: z_recv.at[q], zfold)
        for dist in range(B - 1, 0, -1):
            line(b, B, 1, dist, ysend)

    def inner_all(h):
        for s in range(A):
            for dist in range(B - 1, 0, -1):
                line(b, B, 1, dist, inner_send(h, pick(s)))

    products(cut, tail_rows)
    if A > 1:
        line(a, A, B, A - 1, zsend)
    if early:
        inner_all(0)
    products(0, cut)
    inner_all(len(spans) - 1)
    for dist in range(A - 2, 1, -1):
        line(a, A, B, dist, zsend)
    turn = (len(spans) - 1, 0)
    for h in range(len(spans)):
        for s in range(A - 1):
            outer_step(h, s)
            if (h, s) == (0, 0) and A > 2:
                line(a, A, B, 1, zsend)
            if (h, s) == turn:
                tail_turn()
    if A == 1:
        tail_turn()

    for h in range(len(spans)):
        inner_done(h, a)
        first, rows, parts = spans[h]
        if A > 1:
            for cond, slot in ((a > 0, a + 1), (a < A - 1, a)):
                @pl.when(cond)
                def _(slot=slot, h=h, first=first, rows=rows):
                    at = outb.at[slot, pl.ds(first, rows)]
                    rdma(at, at, o_send.at[h, slot], o_recv.at[h, slot],
                         {"row": mate}).wait_recv()
        if A > 2:
            @pl.when((a > 0) & (a < A - 1))
            def _(first=first, rows=rows):
                at = pl.ds(first, rows)
                outb[a + 1, at] = outb[a + 1, at] + outb[a, at]
        for u, at, lo, n in parts:
            v = here(a, u, at, lo, n)
            if A > 1:
                v = v + outb[near_a, pl.ds(at, n)]
            out_ref[pl.ds(u * side + lo, n), :] = v
    arrive(b, B, lambda q: yb.at[q], lambda q: y_send.at[q], lambda q: y_recv.at[q], yfold)
    last = zhere(b)
    if B > 1:
        last = last + yb[near]
    out_ref[pl.ds(tail, tail_rows), :] = last
    out_first = (me_row * C + me_col) * (piece // lanes)
    for q in range(piece // lanes):
        at = pl.ds(q * lanes, lanes)
        out_ref[at, :] = out_ref[at, :] * factors(out_first + q)

    for group in (directs.values(), mates, forwards.values()):
        for cp in group:
            cp.wait_send()
    for dist in range(A - 1, 0, -1):
        line(a, A, B, dist, lambda t, slot, to, *rest: zcopy(slot, to).wait_send())
    for dist in range(B - 1, 0, -1):
        line(b, B, 1, dist, lambda t, slot, to, *rest: ycopy(slot, to).wait_send())
        for h in range(len(spans)):
            for s in range(A):
                def left(t, slot, to, *rest, h=h, d=pick(s)):
                    inner_copy(h, d, slot, to).wait_send()

                line(b, B, 1, dist, left)
    for h in range(len(spans)):
        for s in range(A - 1):
            outer_copy(h, s)[-1].wait_send()


def sorted_table(count):
    return [sorted(range(count), key=lambda d: (-abs(d - i), -d)) for i in range(count)]


def body(vectors, tile_values, tile_rows, tile_cols, tile_count, degrees):
    R = lax.axis_size("row")
    C = lax.axis_size("col")
    piece, width = vectors.shape
    side = tile_values.shape[-1]
    slots = tile_values.shape[2]
    B = inner_size(C)
    A = C // B
    tpp = piece // side
    chips = R // 2
    dims = (R, A, B, piece, width, side, slots)
    vmem = pl.BlockSpec(memory_space=pltpu.VMEM)
    smem = pl.BlockSpec(memory_space=pltpu.SMEM)
    dma = pltpu.SemaphoreType.DMA
    f32 = jnp.float32
    far = max(chips - 1, 1)
    tail_rows = -(-piece // 96) * 16
    return pl.pallas_call(
        functools.partial(kernel, dims),
        out_shape=jax.ShapeDtypeStruct((piece, width), f32),
        in_specs=[smem, smem, smem, pl.BlockSpec(memory_space=pl.ANY), vmem, pl.BlockSpec(memory_space=pl.ANY)],
        out_specs=vmem,
        scratch_shapes=[
            pltpu.VMEM((slots, side, side), tile_values.dtype),
            pltpu.VMEM((R, piece, width), f32),
            pltpu.VMEM((R * tpp, side, 2 * width), jnp.bfloat16),
            pltpu.VMEM((slots + 1, side, width), f32),
            pltpu.VMEM((A, B + 1, piece - tail_rows, width), f32),
            pltpu.VMEM((A + 1, piece - tail_rows, width), f32),
            pltpu.VMEM((A + 1, B, tail_rows, width), f32),
            pltpu.VMEM((B + 1, tail_rows, width), f32),
            pltpu.SMEM((slots,), jnp.int32),
            pltpu.SMEM((C * tpp,), jnp.int32),
            dma, dma,
            dma((far, tpp)), dma((far, tpp)),
            dma((tpp,)), dma((tpp,)),
            dma((far, tpp)), dma((far, tpp)),
            dma((2, A, B + 1)), dma((2, A, B + 1)),
            dma((2, A + 1)), dma((2, A + 1)),
            dma((A + 1,)), dma((A + 1,)),
            dma((B + 1,)), dma((B + 1,)),
        ],
        compiler_params=pltpu.CompilerParams(
            collective_id=0, has_side_effects=True, vmem_limit_bytes=67043328
        ),
    )(tile_rows, tile_cols, tile_count, vectors, degrees.reshape(-1, 128), tile_values)


def solution(mesh):
    placed = (
        P(("col", "row"), None),
        P("row", "col", None, None, None),
        P("row", "col", None),
        P("row", "col", None),
        P("row", "col"),
        P(),
    )
    return jax.shard_map(
        body, mesh=mesh, in_specs=placed, out_specs=P(("row", "col"), None), check_vma=False
    )
```

```python
import functools

import jax
import jax.numpy as jnp
from jax import lax
from jax.experimental import pallas as pl
from jax.experimental.pallas import tpu as pltpu
from jax.sharding import PartitionSpec as P

MESH = pl.DeviceIdType.MESH


def inner_size(col_count):
    inner = 1
    while inner * inner * 4 <= col_count and col_count % (inner * 2) == 0:
        inner *= 2
    return inner


def kernel(
    dims,
    rows_s, cols_s, count_s, vec_ref, deg_ref, tiles_hbm, out_ref,
    tiles_v, gath, split_v, sums, inb, outb, zb, yb, prev_s, last_s,
    tile_sem, vec_sem, d_send, d_recv, m_send, m_recv, f_send, f_recv,
    i_send, i_recv, o_send, o_recv, z_send, z_recv, y_send, y_recv,
):
    R, A, B, piece, width, side, slots = dims
    C = A * B
    tpp = piece // side
    chips = R // 2
    me_row = lax.axis_index("row")
    me_col = lax.axis_index("col")
    chip, core = me_row // 2, me_row % 2
    mate = chip * 2 + (1 - core)
    a, b = me_col // B, me_col % B
    lanes = 128

    tile_copy = pltpu.make_async_copy(tiles_hbm.at[0, 0], tiles_v, tile_sem)
    tile_copy.start()

    def rdma(src, dst, ssem, rsem, where):
        return pltpu.make_async_remote_copy(
            src_ref=src, dst_ref=dst, send_sem=ssem, recv_sem=rsem,
            device_id=where, device_id_type=MESH,
        )

    barrier = pltpu.get_barrier_semaphore()

    def greet(where):
        pl.semaphore_signal(barrier, inc=1, device_id=where, device_id_type=MESH)

    greet({"row": mate})
    for j in range(1, chips):
        greet({"row": lax.rem(chip + j, chips) * 2 + core})
    conds = []
    if B > 1:
        conds += [(b > 0, me_col - 1), (b < B - 1, me_col + 1)]
    if A > 1:
        conds += [(a > 0, me_col - B), (a < A - 1, me_col + B)]
    for cond, other in conds:
        @pl.when(cond)
        def _(other=other):
            greet({"col": other})
    peers = jnp.int32(chips)
    for cond, other in conds:
        peers = peers + jnp.where(cond, 1, 0)
    pl.semaphore_wait(barrier, peers)

    def part(c):
        return pl.ds(c * side, side)

    directs, mates, forwards = {}, [], {}
    for c in range(tpp):
        for j in range(1, chips):
            dst = lax.rem(chip + j, chips) * 2 + core
            cp = rdma(vec_ref.at[part(c)], gath.at[me_row, part(c)],
                      d_send.at[j - 1, c], d_recv.at[j - 1, c], {"row": dst})
            cp.start()
            directs[j, c] = cp
    for c in range(tpp):
        cp = rdma(vec_ref.at[part(c)], gath.at[me_row, part(c)],
                  m_send.at[c], m_recv.at[c], {"row": mate})
        cp.start()
        mates.append(cp)

    vec_copy = pltpu.make_async_copy(vec_ref, gath.at[me_row], vec_sem)
    vec_copy.start()

    count = count_s[0, 0]

    def link(k, _):
        rk = rows_s[0, 0, k]
        v = jnp.int32(slots)
        for j in range(slots):
            v = jnp.where((rows_s[0, 0, j] == rk) & (j < k), j, v)
        prev_s[k] = v
        return 0

    lax.fori_loop(0, slots, link, 0)

    def ends(r, _):
        v = jnp.int32(slots)
        for j in range(slots):
            v = jnp.where((rows_s[0, 0, j] == r) & (j < count), j, v)
        last_s[r] = v
        return 0

    lax.fori_loop(0, C * tpp, ends, 0)
    sums[slots] = jnp.zeros((side, width), jnp.float32)

    def factors(first):
        d = deg_ref[pl.ds(first, 1), :].astype(jnp.float32)
        return jnp.broadcast_to(lax.rsqrt(d), (lanes, lanes)).T

    col_first = me_col * (R * piece // lanes)

    def scale(get, r, c):
        def step(q, _):
            f = factors(col_first + (r * piece + c * side) // lanes + q)
            x = get(pl.ds(c * side + q * lanes, lanes)) * f
            hi = x.astype(jnp.bfloat16)
            lo = (x - hi.astype(jnp.float32)).astype(jnp.bfloat16)
            at = pl.ds(pl.multiple_of(q * lanes, lanes), lanes)
            split_v[r * tpp + c, at, :width] = hi
            split_v[r * tpp + c, at, width:] = lo
            return 0

        lax.fori_loop(0, side // lanes, step, 0)

    def landed(r, c, ssem, rsem):
        rdma(gath.at[r, part(c)], gath.at[r, part(c)], ssem, rsem, {"row": mate}).wait_recv()

    vec_copy.wait()
    for c in range(tpp):
        scale(lambda s: gath[me_row, s, :], me_row, c)
    for c in range(tpp):
        landed(mate, c, m_send.at[c], m_recv.at[c])
        scale(lambda s: gath[mate, s, :], mate, c)
    for c in range(tpp):
        for j in range(1, chips):
            src = lax.rem(chip - j + chips, chips) * 2 + core
            landed(src, c, d_send.at[j - 1, c], d_recv.at[j - 1, c])
            cp = rdma(gath.at[src, part(c)], gath.at[src, part(c)],
                      f_send.at[j - 1, c], f_recv.at[j - 1, c], {"row": mate})
            cp.start()
            forwards[j, c] = cp
            scale(lambda s, src=src: gath[src, s, :], src, c)
    for c in range(tpp):
        for j in range(1, chips):
            src = lax.rem(chip - j + chips, chips) * 2 + (1 - core)
            landed(src, c, f_send.at[j - 1, c], f_recv.at[j - 1, c])
            scale(lambda s, src=src: gath[src, s, :], src, c)

    tile_copy.wait()

    def products(lo, n):
        def product(k, _):
            both = jnp.dot(tiles_v[k, lo:lo + n], split_v[cols_s[0, 0, k]],
                           preferred_element_type=jnp.float32)
            old = sums[prev_s[k], lo:lo + n]
            sums[k, lo:lo + n] = both[:, :width] + both[:, width:] + old
            return 0

        lax.fori_loop(0, slots, product, 0, unroll=True)

    order = sorted_table(A)
    cut = side - zb.shape[2]
    tail = (tpp - 1) * side + cut
    tail_rows = side - cut
    early = [(u, u * tail_rows, cut, tail_rows) for u in range(tpp - 1)]
    late_at = (tpp - 1) * tail_rows
    late = [(u, late_at + u * cut, 0, cut) for u in range(tpp)]
    spans = [(late_at, tpp * cut, late)]
    if early:
        spans = [(0, late_at, early)] + spans

    def pick(s):
        v = jnp.int32(order[0][s])
        for i in range(1, A):
            v = jnp.where(a == i, order[i][s], v)
        return v

    def own(d, t, u, lo, n):
        return sums[last_s[(d * B + t) * tpp + u], lo:lo + n]

    def own_tail(d, t):
        return sums[last_s[(d * B + t) * tpp + tpp - 1], cut:]

    def line(pos, size, stride, dist, action):
        for right in (True, False):
            t = pos + dist if right else pos - dist
            slot = t + 1 if right else t
            to = me_col + stride if right else me_col - stride
            more = pos > 0 if right else pos < size - 1

            @pl.when((t < size) if right else (t >= 0))
            def _(t=t, slot=slot, to=to, more=more):
                action(t, slot, to, more, dist < size - 1)

    def add_and_send(cp, more, can, store):
        if can:
            @pl.when(more)
            def _():
                cp.wait_recv()
                store(True)

            @pl.when(jnp.logical_not(more))
            def _():
                store(False)
        else:
            store(False)
        cp.start()

    def arrive(pos, size, ref, ssem, rsem, fold):
        if size > 1:
            for cond, slot in ((pos > 0, pos + 1), (pos < size - 1, pos)):
                @pl.when(cond)
                def _(slot=slot):
                    rdma(ref(slot), ref(slot), ssem(slot), rsem(slot), {"row": mate}).wait_recv()
        if size > 2:
            @pl.when((pos > 0) & (pos < size - 1))
            def _():
                fold(pos + 1, pos)

    near = jnp.where(b > 0, b + 1, 0)
    near_a = jnp.where(a > 0, a + 1, 0)

    def inner_copy(h, d, slot, to):
        at = inb.at[d, slot, pl.ds(*spans[h][:2])]
        return rdma(at, at, i_send.at[h, d, slot], i_recv.at[h, d, slot], {"col": to})

    def inner_send(h, d):
        def action(t, slot, to, more, can):
            def store(add):
                for u, at, lo, n in spans[h][2]:
                    rows = pl.ds(at, n)
                    v = own(d, t, u, lo, n)
                    inb[d, slot, rows] = inb[d, slot, rows] + v if add else v

            add_and_send(inner_copy(h, d, slot, to), more, can, store)
        return action

    def inner_done(h, d):
        rows = pl.ds(*spans[h][:2])

        def fold(x, y):
            inb[d, x, rows] = inb[d, x, rows] + inb[d, y, rows]

        arrive(b, B, lambda q: inb.at[d, q, rows], lambda q: i_send.at[h, d, q],
               lambda q: i_recv.at[h, d, q], fold)

    def here(d, u, at, lo, n):
        v = own(d, b, u, lo, n)
        if B > 1:
            v = v + inb[d, near, pl.ds(at, n)]
        return v

    def outer_copy(h, s):
        d = pick(s)
        right = d > a
        slot = jnp.where(right, d + 1, d)
        to = jnp.where(right, me_col + B, me_col - B)
        at = outb.at[slot, pl.ds(*spans[h][:2])]
        return d, right, slot, rdma(at, at, o_send.at[h, slot], o_recv.at[h, slot], {"col": to})

    def outer_step(h, s):
        d, right, slot, cp = outer_copy(h, s)
        inner_done(h, d)
        more = (right & (a > 0)) | (jnp.logical_not(right) & (a < A - 1))

        def store(add):
            for u, at, lo, n in spans[h][2]:
                rows = pl.ds(at, n)
                v = here(d, u, at, lo, n)
                outb[slot, rows] = outb[slot, rows] + v if add else v

        add_and_send(cp, more, True, store)

    def zcopy(slot, to):
        return rdma(zb.at[slot], zb.at[slot], z_send.at[slot], z_recv.at[slot], {"col": to})

    def zsend(d, slot, to, more, can):
        def store(add):
            for t in range(B):
                v = own_tail(d, t)
                zb[slot, t] = zb[slot, t] + v if add else v

        add_and_send(zcopy(slot, to), more, can, store)

    def zhere(t):
        v = own_tail(a, t)
        if A > 1:
            v = v + zb[near_a, t]
        return v

    def ycopy(slot, to):
        return rdma(yb.at[slot], yb.at[slot], y_send.at[slot], y_recv.at[slot], {"col": to})

    def ysend(t, slot, to, more, can):
        def store(add):
            v = zhere(t)
            yb[slot] = yb[slot] + v if add else v

        add_and_send(ycopy(slot, to), more, can, store)

    def zfold(x, y):
        zb[x] = zb[x] + zb[y]

    def yfold(x, y):
        yb[x] = yb[x] + yb[y]

    def tail_turn():
        arrive(a, A, lambda q: zb.at[q], lambda q: z_send.at[q], lambda q: z_recv.at[q], zfold)
        for dist in range(B - 1, 0, -1):
            line(b, B, 1, dist, ysend)

    def inner_all(h):
        for s in range(A):
            for dist in range(B - 1, 0, -1):
                line(b, B, 1, dist, inner_send(h, pick(s)))

    products(cut, tail_rows)
    if A > 1:
        line(a, A, B, A - 1, zsend)
    if early:
        inner_all(0)
    products(0, cut)
    inner_all(len(spans) - 1)
    for dist in range(A - 2, 1, -1):
        line(a, A, B, dist, zsend)
    turn = (len(spans) - 1, 0)
    for h in range(len(spans)):
        for s in range(A - 1):
            outer_step(h, s)
            if (h, s) == (0, 0) and A > 2:
                line(a, A, B, 1, zsend)
            if (h, s) == turn:
                tail_turn()
    if A == 1:
        tail_turn()

    for h in range(len(spans)):
        inner_done(h, a)
        first, rows, parts = spans[h]
        if A > 1:
            for cond, slot in ((a > 0, a + 1), (a < A - 1, a)):
                @pl.when(cond)
                def _(slot=slot, h=h, first=first, rows=rows):
                    at = outb.at[slot, pl.ds(first, rows)]
                    rdma(at, at, o_send.at[h, slot], o_recv.at[h, slot],
                         {"row": mate}).wait_recv()
        if A > 2:
            @pl.when((a > 0) & (a < A - 1))
            def _(first=first, rows=rows):
                at = pl.ds(first, rows)
                outb[a + 1, at] = outb[a + 1, at] + outb[a, at]
        for u, at, lo, n in parts:
            v = here(a, u, at, lo, n)
            if A > 1:
                v = v + outb[near_a, pl.ds(at, n)]
            out_ref[pl.ds(u * side + lo, n), :] = v
    arrive(b, B, lambda q: yb.at[q], lambda q: y_send.at[q], lambda q: y_recv.at[q], yfold)
    last = zhere(b)
    if B > 1:
        last = last + yb[near]
    out_ref[pl.ds(tail, tail_rows), :] = last
    out_first = (me_row * C + me_col) * (piece // lanes)
    for q in range(piece // lanes):
        at = pl.ds(q * lanes, lanes)
        out_ref[at, :] = out_ref[at, :] * factors(out_first + q)

    for group in (directs.values(), mates, forwards.values()):
        for cp in group:
            cp.wait_send()
    for dist in range(A - 1, 0, -1):
        line(a, A, B, dist, lambda t, slot, to, *rest: zcopy(slot, to).wait_send())
    for dist in range(B - 1, 0, -1):
        line(b, B, 1, dist, lambda t, slot, to, *rest: ycopy(slot, to).wait_send())
        for h in range(len(spans)):
            for s in range(A):
                def left(t, slot, to, *rest, h=h, d=pick(s)):
                    inner_copy(h, d, slot, to).wait_send()

                line(b, B, 1, dist, left)
    for h in range(len(spans)):
        for s in range(A - 1):
            outer_copy(h, s)[-1].wait_send()


def sorted_table(count):
    return [sorted(range(count), key=lambda d: (-abs(d - i), -d)) for i in range(count)]


def body(vectors, tile_values, tile_rows, tile_cols, tile_count, degrees):
    R = lax.axis_size("row")
    C = lax.axis_size("col")
    piece, width = vectors.shape
    side = tile_values.shape[-1]
    slots = tile_values.shape[2]
    B = inner_size(C)
    A = C // B
    tpp = piece // side
    chips = R // 2
    dims = (R, A, B, piece, width, side, slots)
    vmem = pl.BlockSpec(memory_space=pltpu.VMEM)
    smem = pl.BlockSpec(memory_space=pltpu.SMEM)
    dma = pltpu.SemaphoreType.DMA
    f32 = jnp.float32
    far = max(chips - 1, 1)
    tail_rows = -(-piece // 96) * 16
    return pl.pallas_call(
        functools.partial(kernel, dims),
        out_shape=jax.ShapeDtypeStruct((piece, width), f32),
        in_specs=[smem, smem, smem, pl.BlockSpec(memory_space=pl.ANY), vmem, pl.BlockSpec(memory_space=pl.ANY)],
        out_specs=vmem,
        scratch_shapes=[
            pltpu.VMEM((slots, side, side), tile_values.dtype),
            pltpu.VMEM((R, piece, width), f32),
            pltpu.VMEM((R * tpp, side, 2 * width), jnp.bfloat16),
            pltpu.VMEM((slots + 1, side, width), f32),
            pltpu.VMEM((A, B + 1, piece - tail_rows, width), f32),
            pltpu.VMEM((A + 1, piece - tail_rows, width), f32),
            pltpu.VMEM((A + 1, B, tail_rows, width), f32),
            pltpu.VMEM((B + 1, tail_rows, width), f32),
            pltpu.SMEM((slots,), jnp.int32),
            pltpu.SMEM((C * tpp,), jnp.int32),
            dma, dma,
            dma((far, tpp)), dma((far, tpp)),
            dma((tpp,)), dma((tpp,)),
            dma((far, tpp)), dma((far, tpp)),
            dma((2, A, B + 1)), dma((2, A, B + 1)),
            dma((2, A + 1)), dma((2, A + 1)),
            dma((A + 1,)), dma((A + 1,)),
            dma((B + 1,)), dma((B + 1,)),
        ],
        compiler_params=pltpu.CompilerParams(
            collective_id=0, has_side_effects=True, vmem_limit_bytes=67043328
        ),
    )(tile_rows, tile_cols, tile_count, vectors, degrees.reshape(-1, 128), tile_values)


def solution(mesh):
    placed = (
        P(("col", "row"), None),
        P("row", "col", None, None, None),
        P("row", "col", None),
        P("row", "col", None),
        P("row", "col"),
        P(),
    )
    return jax.shard_map(
        body, mesh=mesh, in_specs=placed, out_specs=P(("row", "col"), None), check_vma=False
    )
```

```python
import functools

import jax
import jax.numpy as jnp
from jax import lax
from jax.experimental import pallas as pl
from jax.experimental.pallas import tpu as pltpu
from jax.sharding import PartitionSpec as P

MESH = pl.DeviceIdType.MESH


def inner_size(col_count):
    inner = 1
    while inner * inner * 4 <= col_count and col_count % (inner * 2) == 0:
        inner *= 2
    return inner


def kernel(
    dims,
    rows_s, cols_s, count_s, vec_ref, deg_ref, tiles_hbm, out_ref,
    tiles_v, gath, split_v, sums, inb, outb, zb, yb, prev_s, last_s,
    tile_sem, vec_sem, d_send, d_recv, m_send, m_recv, f_send, f_recv,
    i_send, i_recv, o_send, o_recv, z_send, z_recv, y_send, y_recv,
):
    R, A, B, piece, width, side, slots = dims
    C = A * B
    tpp = piece // side
    chips = R // 2
    me_row = lax.axis_index("row")
    me_col = lax.axis_index("col")
    chip, core = me_row // 2, me_row % 2
    mate = chip * 2 + (1 - core)
    a, b = me_col // B, me_col % B
    lanes = 128

    tile_copy = pltpu.make_async_copy(tiles_hbm.at[0, 0], tiles_v, tile_sem)
    tile_copy.start()

    def rdma(src, dst, ssem, rsem, where):
        return pltpu.make_async_remote_copy(
            src_ref=src, dst_ref=dst, send_sem=ssem, recv_sem=rsem,
            device_id=where, device_id_type=MESH,
        )

    barrier = pltpu.get_barrier_semaphore()

    def greet(where):
        pl.semaphore_signal(barrier, inc=1, device_id=where, device_id_type=MESH)

    greet({"row": mate})
    for j in range(1, chips):
        greet({"row": lax.rem(chip + j, chips) * 2 + core})
    conds = []
    if B > 1:
        conds += [(b > 0, me_col - 1), (b < B - 1, me_col + 1)]
    if A > 1:
        conds += [(a > 0, me_col - B), (a < A - 1, me_col + B)]
    for cond, other in conds:
        @pl.when(cond)
        def _(other=other):
            greet({"col": other})
    peers = jnp.int32(chips)
    for cond, other in conds:
        peers = peers + jnp.where(cond, 1, 0)
    pl.semaphore_wait(barrier, peers)

    def part(c):
        return pl.ds(c * side, side)

    directs, mates, forwards = {}, [], {}
    for c in range(tpp):
        for j in range(1, chips):
            dst = lax.rem(chip + j, chips) * 2 + core
            cp = rdma(vec_ref.at[part(c)], gath.at[me_row, part(c)],
                      d_send.at[j - 1, c], d_recv.at[j - 1, c], {"row": dst})
            cp.start()
            directs[j, c] = cp
    for c in range(tpp):
        cp = rdma(vec_ref.at[part(c)], gath.at[me_row, part(c)],
                  m_send.at[c], m_recv.at[c], {"row": mate})
        cp.start()
        mates.append(cp)

    vec_copy = pltpu.make_async_copy(vec_ref, gath.at[me_row], vec_sem)
    vec_copy.start()

    count = count_s[0, 0]

    def link(k, _):
        rk = rows_s[0, 0, k]
        v = jnp.int32(slots)
        for j in range(slots):
            v = jnp.where((rows_s[0, 0, j] == rk) & (j < k), j, v)
        prev_s[k] = v
        return 0

    lax.fori_loop(0, slots, link, 0)

    def ends(r, _):
        v = jnp.int32(slots)
        for j in range(slots):
            v = jnp.where((rows_s[0, 0, j] == r) & (j < count), j, v)
        last_s[r] = v
        return 0

    lax.fori_loop(0, C * tpp, ends, 0)
    sums[slots] = jnp.zeros((side, width), jnp.float32)

    def factors(first):
        d = deg_ref[pl.ds(first, 1), :].astype(jnp.float32)
        return jnp.broadcast_to(lax.rsqrt(d), (lanes, lanes)).T

    col_first = me_col * (R * piece // lanes)

    def scale(get, r, c):
        def step(q, _):
            f = factors(col_first + (r * piece + c * side) // lanes + q)
            x = get(pl.ds(c * side + q * lanes, lanes)) * f
            hi = x.astype(jnp.bfloat16)
            lo = (x - hi.astype(jnp.float32)).astype(jnp.bfloat16)
            at = pl.ds(pl.multiple_of(q * lanes, lanes), lanes)
            split_v[r * tpp + c, at, :width] = hi
            split_v[r * tpp + c, at, width:] = lo
            return 0

        lax.fori_loop(0, side // lanes, step, 0, unroll=True)

    def landed(r, c, ssem, rsem):
        rdma(gath.at[r, part(c)], gath.at[r, part(c)], ssem, rsem, {"row": mate}).wait_recv()

    vec_copy.wait()
    for c in range(tpp):
        scale(lambda s: gath[me_row, s, :], me_row, c)
    for c in range(tpp):
        landed(mate, c, m_send.at[c], m_recv.at[c])
        scale(lambda s: gath[mate, s, :], mate, c)
    for c in range(tpp):
        for j in range(1, chips):
            src = lax.rem(chip - j + chips, chips) * 2 + core
            landed(src, c, d_send.at[j - 1, c], d_recv.at[j - 1, c])
            cp = rdma(gath.at[src, part(c)], gath.at[src, part(c)],
                      f_send.at[j - 1, c], f_recv.at[j - 1, c], {"row": mate})
            cp.start()
            forwards[j, c] = cp
            scale(lambda s, src=src: gath[src, s, :], src, c)
    for c in range(tpp):
        for j in range(1, chips):
            src = lax.rem(chip - j + chips, chips) * 2 + (1 - core)
            landed(src, c, f_send.at[j - 1, c], f_recv.at[j - 1, c])
            scale(lambda s, src=src: gath[src, s, :], src, c)

    tile_copy.wait()

    def products(lo, n):
        def product(k, _):
            both = jnp.dot(tiles_v[k, lo:lo + n], split_v[cols_s[0, 0, k]],
                           preferred_element_type=jnp.float32)
            old = sums[prev_s[k], lo:lo + n]
            sums[k, lo:lo + n] = both[:, :width] + both[:, width:] + old
            return 0

        lax.fori_loop(0, slots, product, 0, unroll=True)

    order = sorted_table(A)
    cut = side - zb.shape[2]
    tail = (tpp - 1) * side + cut
    tail_rows = side - cut
    early = [(u, u * tail_rows, cut, tail_rows) for u in range(tpp - 1)]
    late_at = (tpp - 1) * tail_rows
    late = [(u, late_at + u * cut, 0, cut) for u in range(tpp)]
    spans = [(late_at, tpp * cut, late)]
    if early:
        spans = [(0, late_at, early)] + spans

    def pick(s):
        v = jnp.int32(order[0][s])
        for i in range(1, A):
            v = jnp.where(a == i, order[i][s], v)
        return v

    def own(d, t, u, lo, n):
        return sums[last_s[(d * B + t) * tpp + u], lo:lo + n]

    def own_tail(d, t):
        return sums[last_s[(d * B + t) * tpp + tpp - 1], cut:]

    def line(pos, size, stride, dist, action):
        for right in (True, False):
            t = pos + dist if right else pos - dist
            slot = t + 1 if right else t
            to = me_col + stride if right else me_col - stride
            more = pos > 0 if right else pos < size - 1

            @pl.when((t < size) if right else (t >= 0))
            def _(t=t, slot=slot, to=to, more=more):
                action(t, slot, to, more, dist < size - 1)

    def add_and_send(cp, more, can, store):
        if can:
            @pl.when(more)
            def _():
                cp.wait_recv()
                store(True)

            @pl.when(jnp.logical_not(more))
            def _():
                store(False)
        else:
            store(False)
        cp.start()

    def arrive(pos, size, ref, ssem, rsem, fold):
        if size > 1:
            for cond, slot in ((pos > 0, pos + 1), (pos < size - 1, pos)):
                @pl.when(cond)
                def _(slot=slot):
                    rdma(ref(slot), ref(slot), ssem(slot), rsem(slot), {"row": mate}).wait_recv()
        if size > 2:
            @pl.when((pos > 0) & (pos < size - 1))
            def _():
                fold(pos + 1, pos)

    near = jnp.where(b > 0, b + 1, 0)
    near_a = jnp.where(a > 0, a + 1, 0)

    def inner_copy(h, d, slot, to):
        at = inb.at[d, slot, pl.ds(*spans[h][:2])]
        return rdma(at, at, i_send.at[h, d, slot], i_recv.at[h, d, slot], {"col": to})

    def inner_send(h, d):
        def action(t, slot, to, more, can):
            def store(add):
                for u, at, lo, n in spans[h][2]:
                    rows = pl.ds(at, n)
                    v = own(d, t, u, lo, n)
                    inb[d, slot, rows] = inb[d, slot, rows] + v if add else v

            add_and_send(inner_copy(h, d, slot, to), more, can, store)
        return action

    def inner_done(h, d):
        rows = pl.ds(*spans[h][:2])

        def fold(x, y):
            inb[d, x, rows] = inb[d, x, rows] + inb[d, y, rows]

        arrive(b, B, lambda q: inb.at[d, q, rows], lambda q: i_send.at[h, d, q],
               lambda q: i_recv.at[h, d, q], fold)

    def here(d, u, at, lo, n):
        v = own(d, b, u, lo, n)
        if B > 1:
            v = v + inb[d, near, pl.ds(at, n)]
        return v

    def outer_copy(h, s):
        d = pick(s)
        right = d > a
        slot = jnp.where(right, d + 1, d)
        to = jnp.where(right, me_col + B, me_col - B)
        at = outb.at[slot, pl.ds(*spans[h][:2])]
        return d, right, slot, rdma(at, at, o_send.at[h, slot], o_recv.at[h, slot], {"col": to})

    def outer_step(h, s):
        d, right, slot, cp = outer_copy(h, s)
        inner_done(h, d)
        more = (right & (a > 0)) | (jnp.logical_not(right) & (a < A - 1))

        def store(add):
            for u, at, lo, n in spans[h][2]:
                rows = pl.ds(at, n)
                v = here(d, u, at, lo, n)
                outb[slot, rows] = outb[slot, rows] + v if add else v

        add_and_send(cp, more, True, store)

    def zcopy(slot, to):
        return rdma(zb.at[slot], zb.at[slot], z_send.at[slot], z_recv.at[slot], {"col": to})

    def zsend(d, slot, to, more, can):
        def store(add):
            for t in range(B):
                v = own_tail(d, t)
                zb[slot, t] = zb[slot, t] + v if add else v

        add_and_send(zcopy(slot, to), more, can, store)

    def zhere(t):
        v = own_tail(a, t)
        if A > 1:
            v = v + zb[near_a, t]
        return v

    def ycopy(slot, to):
        return rdma(yb.at[slot], yb.at[slot], y_send.at[slot], y_recv.at[slot], {"col": to})

    def ysend(t, slot, to, more, can):
        def store(add):
            v = zhere(t)
            yb[slot] = yb[slot] + v if add else v

        add_and_send(ycopy(slot, to), more, can, store)

    def zfold(x, y):
        zb[x] = zb[x] + zb[y]

    def yfold(x, y):
        yb[x] = yb[x] + yb[y]

    def tail_turn():
        arrive(a, A, lambda q: zb.at[q], lambda q: z_send.at[q], lambda q: z_recv.at[q], zfold)
        for dist in range(B - 1, 0, -1):
            line(b, B, 1, dist, ysend)

    def inner_all(h):
        for s in range(A):
            for dist in range(B - 1, 0, -1):
                line(b, B, 1, dist, inner_send(h, pick(s)))

    products(cut, tail_rows)
    if A > 1:
        line(a, A, B, A - 1, zsend)
    if early:
        inner_all(0)
    products(0, cut)
    inner_all(len(spans) - 1)
    for dist in range(A - 2, 1, -1):
        line(a, A, B, dist, zsend)
    turn = (len(spans) - 1, 0)
    for h in range(len(spans)):
        for s in range(A - 1):
            outer_step(h, s)
            if (h, s) == (0, 0) and A > 2:
                line(a, A, B, 1, zsend)
            if (h, s) == turn:
                tail_turn()
    if A == 1:
        tail_turn()

    for h in range(len(spans)):
        inner_done(h, a)
        first, rows, parts = spans[h]
        if A > 1:
            for cond, slot in ((a > 0, a + 1), (a < A - 1, a)):
                @pl.when(cond)
                def _(slot=slot, h=h, first=first, rows=rows):
                    at = outb.at[slot, pl.ds(first, rows)]
                    rdma(at, at, o_send.at[h, slot], o_recv.at[h, slot],
                         {"row": mate}).wait_recv()
        if A > 2:
            @pl.when((a > 0) & (a < A - 1))
            def _(first=first, rows=rows):
                at = pl.ds(first, rows)
                outb[a + 1, at] = outb[a + 1, at] + outb[a, at]
        for u, at, lo, n in parts:
            v = here(a, u, at, lo, n)
            if A > 1:
                v = v + outb[near_a, pl.ds(at, n)]
            out_ref[pl.ds(u * side + lo, n), :] = v
    arrive(b, B, lambda q: yb.at[q], lambda q: y_send.at[q], lambda q: y_recv.at[q], yfold)
    last = zhere(b)
    if B > 1:
        last = last + yb[near]
    out_ref[pl.ds(tail, tail_rows), :] = last
    out_first = (me_row * C + me_col) * (piece // lanes)
    for q in range(piece // lanes):
        at = pl.ds(q * lanes, lanes)
        out_ref[at, :] = out_ref[at, :] * factors(out_first + q)

    for group in (directs.values(), mates, forwards.values()):
        for cp in group:
            cp.wait_send()
    for dist in range(A - 1, 0, -1):
        line(a, A, B, dist, lambda t, slot, to, *rest: zcopy(slot, to).wait_send())
    for dist in range(B - 1, 0, -1):
        line(b, B, 1, dist, lambda t, slot, to, *rest: ycopy(slot, to).wait_send())
        for h in range(len(spans)):
            for s in range(A):
                def left(t, slot, to, *rest, h=h, d=pick(s)):
                    inner_copy(h, d, slot, to).wait_send()

                line(b, B, 1, dist, left)
    for h in range(len(spans)):
        for s in range(A - 1):
            outer_copy(h, s)[-1].wait_send()


def sorted_table(count):
    return [sorted(range(count), key=lambda d: (-abs(d - i), -d)) for i in range(count)]


def body(vectors, tile_values, tile_rows, tile_cols, tile_count, degrees):
    R = lax.axis_size("row")
    C = lax.axis_size("col")
    piece, width = vectors.shape
    side = tile_values.shape[-1]
    slots = tile_values.shape[2]
    B = inner_size(C)
    A = C // B
    tpp = piece // side
    chips = R // 2
    dims = (R, A, B, piece, width, side, slots)
    vmem = pl.BlockSpec(memory_space=pltpu.VMEM)
    smem = pl.BlockSpec(memory_space=pltpu.SMEM)
    dma = pltpu.SemaphoreType.DMA
    f32 = jnp.float32
    far = max(chips - 1, 1)
    tail_rows = -(-piece // 96) * 16
    return pl.pallas_call(
        functools.partial(kernel, dims),
        out_shape=jax.ShapeDtypeStruct((piece, width), f32),
        in_specs=[smem, smem, smem, pl.BlockSpec(memory_space=pl.ANY), vmem, pl.BlockSpec(memory_space=pl.ANY)],
        out_specs=vmem,
        scratch_shapes=[
            pltpu.VMEM((slots, side, side), tile_values.dtype),
            pltpu.VMEM((R, piece, width), f32),
            pltpu.VMEM((R * tpp, side, 2 * width), jnp.bfloat16),
            pltpu.VMEM((slots + 1, side, width), f32),
            pltpu.VMEM((A, B + 1, piece - tail_rows, width), f32),
            pltpu.VMEM((A + 1, piece - tail_rows, width), f32),
            pltpu.VMEM((A + 1, B, tail_rows, width), f32),
            pltpu.VMEM((B + 1, tail_rows, width), f32),
            pltpu.SMEM((slots,), jnp.int32),
            pltpu.SMEM((C * tpp,), jnp.int32),
            dma, dma,
            dma((far, tpp)), dma((far, tpp)),
            dma((tpp,)), dma((tpp,)),
            dma((far, tpp)), dma((far, tpp)),
            dma((2, A, B + 1)), dma((2, A, B + 1)),
            dma((2, A + 1)), dma((2, A + 1)),
            dma((A + 1,)), dma((A + 1,)),
            dma((B + 1,)), dma((B + 1,)),
        ],
        compiler_params=pltpu.CompilerParams(
            collective_id=0, has_side_effects=True, vmem_limit_bytes=67043328
        ),
    )(tile_rows, tile_cols, tile_count, vectors, degrees.reshape(-1, 128), tile_values)


def solution(mesh):
    placed = (
        P(("col", "row"), None),
        P("row", "col", None, None, None),
        P("row", "col", None),
        P("row", "col", None),
        P("row", "col"),
        P(),
    )
    return jax.shard_map(
        body, mesh=mesh, in_specs=placed, out_specs=P(("row", "col"), None), check_vma=False
    )
```
